128 devices in a mesh: bins: 64 (over x, y, z), diag: 2 (over core).
Axes of the slice: x: 4, y: 4, z: 4, core: 2. Of those that a mesh axis runs over, the one named last changes fastest.
Arguments:
- held_tiles: float32 [128, 2, 1024, 1024], P('bins', 'diag'), may hold values from 0.01 to 20, as said below
- placed: int32 [128], P('bins'), may hold values from 0 to 1, as said below
- bin_mask: int32 [131072], P('bins'), may hold values 0 or 1
- bias: float32 [131072], P('bins'), may hold values from 0.5 to 2
Outputs:
- balanced: float32 [128, 2, 1024, 1024], P('bins', 'diag')
- bias_out: float32 [131072], P('bins')
The draws below stay inside these ranges and needn't reach their ends.
Inputs may be any that keep to these rules, and one draw needn't show every extreme that they name: placed[q] equals placed[(q + 64) mod 128]; placed[q] is 1 where q is a multiple of 2. `held_tiles`: entries are positive.
All inputs are finite; a program needn't handle non-finite values. No bound on the sum of `bin_mask` on one device may be relied on, other than what follows from the above.
Results may differ from the reference program's by a relative error of at most 0.00012.
Values sent between devices are 32-bit elements; how exact they have to be, the bound alone decides.
No kernel may reach another device: no remote copies, remote signals or barrier semaphores. Data moves between devices by JAX's collectives and lax.ppermute only.
A program may use at most 128 MiB of HBM per device.

```python
import math
import jax
import jax.numpy as jnp

TILE = 1024
TILES_DEV = 2
ITERS = 2
TILE_ROWS = 128
BINS = 131072


def draw_placed(key, part):
    half_flags = jax.random.randint(jax.random.fold_in(key, 11), (TILE_ROWS // 2,), 0, 2).astype(jnp.int32)
    first_rows = jnp.arange(TILE_ROWS // 2, dtype=jnp.int32) % TILES_DEV == 0
    half_flags = jnp.where(first_rows, 1, half_flags).astype(jnp.int32)
    return jnp.concatenate([half_flags, half_flags])


def draw_held_tiles(key, part):
    lines = jnp.arange(TILE, dtype=jnp.float32)
    offsets = jnp.arange(2, dtype=jnp.float32)
    distance = jnp.abs(offsets[:, None, None] * TILE + lines[None, None, :] - lines[None, :, None])
    decay = 1.0 / (1.0 + distance / 256.0)
    position = jnp.arange(TILE_ROWS, dtype=jnp.float32) / max(TILE_ROWS - 1, 1)
    shape = (TILE_ROWS, 2, TILE, TILE)
    noise = jnp.exp(jax.random.uniform(jax.random.fold_in(key, 22), shape, jnp.float32, -1.0, 1.0))
    rise = 1.0 + 2.0 * position
    return (noise * decay[None] * rise[:, None, None, None]).astype(jnp.float32)


def plant(drawn, stream_key, smallest, high):
    index_at = [jax.random.randint(jax.random.fold_in(stream_key, axis), (), 0, length) for axis, length in enumerate(drawn.shape)]
    longest = drawn.shape.index(max(drawn.shape))
    neighbour = index_at[:longest] + [(index_at[longest] + 1) % drawn.shape[longest]] + index_at[longest + 1:]
    return drawn.at[tuple(index_at)].set(smallest).at[tuple(neighbour)].set(high)


def block_scale(rng, extent, cuts, least, high):
    factor_of, own = 1.0, jax.random.fold_in(rng, 6)
    for axis_at, blocks in cuts:
        heights = jnp.exp(jax.random.uniform(jax.random.fold_in(own, axis_at), (blocks,), jnp.float32, least / len(cuts), high / len(cuts)))
        factor_of = factor_of * jnp.repeat(heights, extent[axis_at] // blocks).reshape([-1 if axis == axis_at else 1 for axis in range(len(extent))])
    return factor_of


def setup_inputs(seed: int = 0) -> dict:
    seeds = jax.random.split(jax.random.key(seed), 5)
    return {
        "held_tiles": draw_held_tiles(jax.random.fold_in(seeds[4], 71), 0),
        "placed": draw_placed(jax.random.fold_in(seeds[4], 71), 0),
        "bin_mask": plant((jax.random.randint(seeds[2], (BINS,), 0, 10) < 9).astype(jnp.int32), jax.random.fold_in(seeds[2], 1), 0, 1),
        "bias": jnp.clip(jnp.exp(math.log(2.0) - 1.3862944 * jax.random.uniform(seeds[3], (BINS,), jnp.float32) ** block_scale(seeds[3], (BINS,), ((0, 64),), -0.2, 0.2)), 0.5, 2.0),
    }


def reference(held_tiles, placed, bin_mask, bias):
    row_index = jnp.arange(TILE_ROWS, dtype=jnp.int32)
    partner = (row_index + TILE_ROWS // 2) % TILE_ROWS
    source = jnp.where(placed == 1, partner, row_index).astype(jnp.int32)
    home_tiles = held_tiles[source]
    live = bin_mask.astype(jnp.float32).reshape(TILE_ROWS, TILE)
    empty_row = jnp.zeros((1, TILE), jnp.float32)
    live_next = jnp.concatenate([live[1:], empty_row], axis=0)
    lines = jnp.arange(TILE, dtype=jnp.int32)
    upper_mask = (lines[:, None] <= lines[None, :]).astype(jnp.float32)
    diag_block = home_tiles[:, 0] * upper_mask * live[:, :, None] * live[:, None, :]
    off_block = home_tiles[:, 1] * live[:, :, None] * live_next[:, None, :]
    bias_now = bias.reshape(TILE_ROWS, TILE)
    for repeat in range(ITERS):
        row_diag = jnp.sum(diag_block, axis=2)
        col_diag = jnp.sum(diag_block, axis=1) - jnp.diagonal(diag_block, axis1=1, axis2=2)
        row_off = jnp.sum(off_block, axis=2)
        col_off = jnp.sum(off_block, axis=1)
        sums = row_diag + col_diag + row_off + jnp.concatenate([empty_row, col_off[:-1]], axis=0)
        masked_total = jnp.sum(sums * live)
        live_count = jnp.sum(live)
        mean_sum = masked_total / live_count
        factor = jnp.where(live > 0, sums / mean_sum, 1.0)
        bias_now = bias_now * factor
        inverse = 1.0 / factor
        inverse_next = jnp.concatenate([inverse[1:], empty_row], axis=0)
        diag_block = diag_block * inverse[:, :, None] * inverse[:, None, :]
        off_block = off_block * inverse[:, :, None] * inverse_next[:, None, :]
    balanced = jnp.stack([diag_block, off_block], axis=1)
    return balanced, bias_now.reshape(BINS)
```

```python
import functools

import jax
import jax.numpy as jnp
from jax import lax
from jax.experimental import pallas as pl
from jax.experimental.pallas import tpu as pltpu
from jax.sharding import PartitionSpec as P

AXES = ("bins", "diag")
F32 = jnp.float32
LANE = 128
VMEM_LIMIT = 48 * 1024 * 1024


def iotas():
    rows = lax.broadcasted_iota(jnp.int32, (LANE, LANE), 0)
    cols = lax.broadcasted_iota(jnp.int32, (LANE, LANE), 1)
    return rows, cols


def as_column(line):
    return jnp.broadcast_to(line, (LANE, LANE)).T


def lanes(k):
    return pl.ds(k * LANE, LANE)


def moves(n_bins):
    half = n_bins // 2

    def send(value, pairs):
        return lax.ppermute(value, AXES, pairs)

    chips = range(n_bins)
    down = [(2 * d, 2 * d + 1) for d in chips]
    up = [(2 * d + 1, 2 * d) for d in chips]
    across = [(2 * d, 2 * ((d + half) % n_bins)) for d in chips]
    tiles = [(2 * d + 1, 2 * ((d + half) % n_bins) + 1) for d in chips]
    relayed = [(2 * d + 1, 2 * ((d + half) % n_bins)) for d in chips]
    before = [(2 * d + 2, 2 * d) for d in range(n_bins - 1)]
    after = [(2 * d, 2 * d + 2) for d in range(n_bins - 1)]
    names = dict(down=down, up=up, across=across, tiles=tiles, relayed=relayed, before=before, after=after)
    out = {name: functools.partial(send, pairs=pairs) for name, pairs in names.items()}

    def total(value):
        step = 1
        while step < n_bins:
            value = value + send(value, [(2 * d, 2 * (d ^ step)) for d in chips])
            step *= 2
        return value

    out["total"] = total
    return out


def pack_place(s):
    t = jnp.where((s >= 1) & (s <= 4), 0, 1)
    k = jnp.where(s == 0, 0, jnp.where(s <= 4, s - 1, s - 4))
    return t, k


def pack_kernel(near_ref, far_ref, most_ref, last_ref, dv_ref):
    s = pl.program_id(0)
    _, k_now = pack_place(s)
    rows, cols = iotas()

    def fill(to_ref, k):
        far = far_ref[0, 0, :, lanes(7 - k)]
        near = near_ref[0, 0, :, lanes(k)]
        to_ref[:, lanes(k)] = jnp.where(cols >= rows, near, far.T)
        dv_ref[0] = jnp.sum(jnp.where(cols == rows, far, 0.0), axis=0, keepdims=True)
        for j in range(k + 1, 8):
            to_ref[:, lanes(j)] = near_ref[0, 0, :, lanes(j)]
        for j in range(k):
            to_ref[:, lanes(j)] = far_ref[0, 0, :, lanes(8 - k + j)]

    @pl.when(s == 0)
    def _():
        fill(last_ref, 0)

    for k in range(4):
        @pl.when((s > 0) & (k_now == k))
        def _():
            fill(most_ref, k)


def pack(held):
    block = (1, 1, LANE, 1024)
    return pl.pallas_call(
        pack_kernel,
        grid=(8,),
        in_specs=[
            pl.BlockSpec(block, lambda s: (pack_place(s)[0], 0, pack_place(s)[1], 0)),
            pl.BlockSpec(block, lambda s: (pack_place(s)[0], 0, 7 - pack_place(s)[1], 0)),
        ],
        out_specs=[
            pl.BlockSpec((LANE, 1024), lambda s: (jnp.maximum(s - 1, 0), 0)),
            pl.BlockSpec((LANE, 1024), lambda s: (0, 0)),
            pl.BlockSpec((1, 1, LANE), lambda s: (s, 0, 0)),
        ],
        out_shape=[
            jax.ShapeDtypeStruct((7 * LANE, 1024), F32),
            jax.ShapeDtypeStruct((LANE, 1024), F32),
            jax.ShapeDtypeStruct((8, 1, LANE), F32),
        ],
        compiler_params=pltpu.CompilerParams(vmem_limit_bytes=VMEM_LIMIT),
        cost_estimate=pl.CostEstimate(flops=1 << 20, bytes_accessed=12 << 20, transcendentals=0),
        name="pack_triangles",
    )(held, held)


ROWS = 256


def sums_kernel(sc_ref, x_ref, a_ref, b_ref, row_ref, col_ref):
    i = pl.program_id(1)
    rows, cols = iotas()
    ahead = cols - rows
    on_diagonal = sc_ref[0] == 1
    least = jnp.where(on_diagonal, 0, -4096)
    least_col = jnp.where(on_diagonal, 1, -4096)

    @pl.when(i == 0)
    def _():
        col_ref[...] = jnp.zeros_like(col_ref)

    for r in range(ROWS // LANE):
        a_line = a_ref[0, :, lanes(r)]
        a_col = as_column(a_line)
        start = i * ROWS + r * LANE
        across = jnp.zeros((LANE, LANE), F32)
        for k in range(8):
            x = x_ref[0, 0, pl.ds(r * LANE, LANE), lanes(k)]
            shift = start - k * LANE
            b_line = b_ref[0, :, lanes(k)]
            across += jnp.where(ahead >= least + shift, x, 0.0) * b_line
            down = jnp.where(ahead >= least_col + shift, x, 0.0) * a_col
            col_ref[0, :, lanes(k)] += jnp.sum(down, axis=0, keepdims=True)
        row_ref[0, :, lanes(r)] = jnp.sum(across.T, axis=0, keepdims=True) * a_line

    @pl.when(i == pl.num_programs(1) - 1)
    def _():
        col_ref[...] *= b_ref[...]


def weighted_sums(scalars, held, row_w, col_w):
    steps = 1024 // ROWS
    shape = jax.ShapeDtypeStruct((2, 1, 1024), F32)
    row_part, col_part = pl.pallas_call(
        sums_kernel,
        grid_spec=pltpu.PrefetchScalarGridSpec(
            num_scalar_prefetch=1,
            grid=(2, steps),
            in_specs=[
                pl.BlockSpec((1, 1, ROWS, 1024), lambda t, i, sc: (t, 0, i, 0)),
                pl.BlockSpec((1, 1, ROWS), lambda t, i, sc: (t, 0, i)),
                pl.BlockSpec((1, 1, 1024), lambda t, i, sc: (t, 0, 0)),
            ],
            out_specs=[
                pl.BlockSpec((1, 1, ROWS), lambda t, i, sc: (t, 0, i)),
                pl.BlockSpec((1, 1, 1024), lambda t, i, sc: (t, 0, 0)),
            ],
        ),
        out_shape=[shape, shape],
        compiler_params=pltpu.CompilerParams(vmem_limit_bytes=VMEM_LIMIT),
        cost_estimate=pl.CostEstimate(flops=8 << 20, bytes_accessed=8 << 20, transcendentals=0),
        name="weighted_sums",
    )(scalars, held, row_w.reshape(2, 1, 1024), col_w.reshape(2, 1, 1024))
    return row_part.reshape(2, 1024), col_part.reshape(2, 1024)


def most_place(i):
    t = jnp.where(i < 8, 0, 1)
    k = jnp.where(i < 8, i // 2, (i - 8) // 2 + 1)
    return t, k, jnp.where(i % 2 == 0, k, 7 - k)


def last_place(i):
    return 1, 0, jnp.where(i == 0, 0, 7)


def balance_kernel(place, sc_ref, got_ref, held_ref, pk_ref, dv_ref, wr_ref, wc_ref, *rest):
    out_ref = rest[-1]
    t, k_now, b = place(pl.program_id(0))
    rows, cols = iotas()
    on_diagonal = sc_ref[0] == 1
    moved = sc_ref[1 + t] == 1
    w_col = as_column(wr_ref[0])

    def put(j, x):
        out_ref[0, 0, :, lanes(j)] = x * w_col * wc_ref[0, :, lanes(j)]

    @pl.when(moved & jnp.logical_not(on_diagonal))
    def _():
        for j in range(8):
            put(j, got_ref[0, 0, :, lanes(j)])

    @pl.when(jnp.logical_not(moved))
    def _():
        least = jnp.where(on_diagonal, 0, -4096) + b * LANE
        for j in range(8):
            put(j, jnp.where(cols - rows >= least - j * LANE, held_ref[0, 0, :, lanes(j)], 0.0))

    for k in range(4):
        @pl.when(moved & on_diagonal & (k_now == k) & (b == k))
        def _():
            for j in range(k):
                out_ref[0, 0, :, lanes(j)] = jnp.zeros((LANE, LANE), F32)
            put(k, jnp.where(cols >= rows, pk_ref[:, lanes(k)], 0.0))
            for j in range(k + 1, 8):
                put(j, pk_ref[:, lanes(j)])

        @pl.when(moved & on_diagonal & (k_now == k) & (b == 7 - k))
        def _():
            for j in range(7 - k):
                out_ref[0, 0, :, lanes(j)] = jnp.zeros((LANE, LANE), F32)
            far = pk_ref[:, lanes(k)].T
            put(7 - k, jnp.where(cols > rows, far, jnp.where(cols == rows, dv_ref[0], 0.0)))
            for j in range(k):
                put(8 - k + j, pk_ref[:, lanes(j)])


def balance(place, steps, packed_row, scalars, got, held, packed, dv, wr, wc, into=None):
    tile = (1, 1, LANE, 1024)

    def got_at(i, sc):
        t, _, b = place(i)
        use = (sc[0] == 0) & (sc[1 + t] == 1)
        return (jnp.where(use, t, 0), 0, jnp.where(use, b, 0), 0)

    def held_at(i, sc):
        t, _, b = place(i)
        use = sc[1 + t] == 0
        return (jnp.where(use, t, 0), 0, jnp.where(use, b, 0), 0)

    def packed_at(i, sc):
        t, k, _ = place(i)
        use = (sc[0] == 1) & (sc[1 + t] == 1)
        return (jnp.where(use, packed_row(t, k), 0), 0)

    def dv_at(i, sc):
        t, k, _ = place(i)
        return (jnp.where(t == 0, 1 + k, jnp.where(k == 0, 0, 4 + k)), 0, 0)

    in_specs = [
        pl.BlockSpec(tile, got_at),
        pl.BlockSpec(tile, held_at),
        pl.BlockSpec((LANE, 1024), packed_at),
        pl.BlockSpec((1, 1, LANE), dv_at),
        pl.BlockSpec((1, 1, LANE), lambda i, sc: (place(i)[0] * 8 + place(i)[2], 0, 0)),
        pl.BlockSpec((1, 1, 1024), lambda i, sc: (place(i)[0], 0, 0)),
    ]
    args = [scalars, got, held, packed, dv, wr, wc]
    aliases = {}
    if into is not None:
        in_specs.append(pl.BlockSpec(memory_space=pl.ANY))
        args.append(into)
        aliases = {len(args) - 1: 0}
    return pl.pallas_call(
        functools.partial(balance_kernel, place),
        grid_spec=pltpu.PrefetchScalarGridSpec(
            num_scalar_prefetch=1,
            grid=(steps,),
            in_specs=in_specs,
            out_specs=pl.BlockSpec(tile, lambda i, sc: (place(i)[0], 0, place(i)[2], 0)),
        ),
        out_shape=jax.ShapeDtypeStruct(held.shape, F32),
        input_output_aliases=aliases,
        compiler_params=pltpu.CompilerParams(vmem_limit_bytes=VMEM_LIMIT),
        cost_estimate=pl.CostEstimate(flops=steps << 18, bytes_accessed=steps << 20, transcendentals=0),
        name="balance_most" if into is None else "balance_last",
    )(*args)


def local(held_tiles, placed, bin_mask, bias):
    move = moves(lax.axis_size("bins"))
    on_diagonal = lax.axis_index("diag") == 0
    live = bin_mask.astype(F32).reshape(2, 1024)
    alive = live > 0
    flags = (placed == 1)[:, None]
    scalars = jnp.concatenate([on_diagonal.astype(jnp.int32)[None], (placed == 1).astype(jnp.int32)])

    got = move["tiles"](held_tiles)
    most, last, dv = pack(held_tiles)
    most = move["relayed"](move["down"](most))
    last = move["relayed"](move["down"](last))

    def as_stored(lines):
        own = jnp.concatenate([lines, move["before"](lines[0:1])], axis=0)
        theirs = move["across"](own)
        rows = jnp.where(flags, theirs[:2], own[:2])
        cols = jnp.where(flags, theirs[1:], own[1:])
        passed = move["down"](jnp.concatenate([rows, cols], axis=0))
        return jnp.where(on_diagonal, rows, passed[:2]), jnp.where(on_diagonal, rows, passed[2:])

    def home_sums(row_w, col_w):
        row_part, col_part = weighted_sums(scalars, held_tiles, row_w, col_w)
        off = move["up"](jnp.concatenate([row_part, col_part], axis=0))
        stored = jnp.concatenate([row_part + col_part + off[:2], off[2:]], axis=0)
        parts = jnp.where(jnp.concatenate([flags, flags], axis=0), move["across"](stored), stored)
        return parts[:2] + jnp.concatenate([move["after"](parts[3:4]), parts[2:3]], axis=0)

    sums_1 = home_sums(*as_stored(live))
    inverse_1 = jnp.where(alive, 1.0 / sums_1, 0.0)
    sums_2 = home_sums(*as_stored(inverse_1))
    inverse = jnp.where(alive, inverse_1 / sums_2, 0.0)
    following = move["before"](inverse[0:1])
    both = [jnp.sum(sums_1 * live), jnp.sum(sums_2 * live), jnp.sum(live)]
    totals = move["total"](jnp.pad(jnp.stack(both)[None], ((0, 0), (0, LANE - 3))))
    mean_1, mean_2 = totals[0, 0] / totals[0, 2], totals[0, 1] / totals[0, 2]
    lines = jnp.concatenate([inverse, following], axis=0)
    weights = jnp.where(lines > 0, lines * (mean_1 * mean_2), 0.0)
    factor = jnp.where(alive, (sums_1 / mean_1) * (sums_2 / mean_2), 1.0)
    result = jnp.concatenate([weights, factor], axis=0)
    result = jnp.where(on_diagonal, result, move["down"](result))
    bias_out = bias.reshape(2, 1024) * result[3:]
    wr = result[:2].reshape(16, 1, LANE)
    wc = jnp.where(on_diagonal, result[:2], result[1:3]).reshape(2, 1, 1024)
    dv = move["across"](dv)

    got, most, wr, wc, dv = lax.optimization_barrier((got, most, wr, wc, dv))
    out = balance(most_place, 14, lambda t, k: k + 3 * t, scalars, got, held_tiles, most, dv, wr, wc)
    out, last = lax.optimization_barrier((out, last))
    out = balance(last_place, 2, lambda t, k: 0, scalars, got, held_tiles, last, dv, wr, wc, into=out)
    return out, bias_out.reshape(2048)


def solution(mesh):
    placed = (P("bins", "diag", None, None), P("bins"), P("bins"), P("bins"))
    return jax.shard_map(
        local,
        mesh=mesh,
        in_specs=placed,
        out_specs=(P("bins", "diag", None, None), P("bins")),
        check_vma=False,
    )
```

```python
import functools

import jax
import jax.numpy as jnp
from jax import lax
from jax.experimental import pallas as pl
from jax.experimental.pallas import tpu as pltpu
from jax.sharding import PartitionSpec as P

AXES = ("bins", "diag")
F32 = jnp.float32
LANE = 128
VMEM_LIMIT = 48 * 1024 * 1024


def iotas():
    rows = lax.broadcasted_iota(jnp.int32, (LANE, LANE), 0)
    cols = lax.broadcasted_iota(jnp.int32, (LANE, LANE), 1)
    return rows, cols


def as_column(line):
    return jnp.broadcast_to(line, (LANE, LANE)).T


def lanes(k):
    return pl.ds(k * LANE, LANE)


def moves(n_bins):
    half = n_bins // 2
    chips = range(n_bins)

    def other(d):
        return (d + half) % n_bins

    def move(pairs, source_core, target_core):
        pairs = [(2 * s + source_core, 2 * t + target_core) for s, t in pairs]
        return lambda value: lax.ppermute(value, AXES, pairs)

    plane = max(n_bins // 4, 1)
    planes = [list(range(start, start + plane)) for start in range(0, n_bins, plane)]

    def plane_sum(value):
        spread = jnp.broadcast_to(value, (plane, value.shape[1]))
        seen = lax.all_to_all(spread, "bins", 0, 0, axis_index_groups=planes, tiled=True)
        return jnp.sum(seen, axis=0, keepdims=True)

    same = [(d, d) for d in chips]
    swap = [(d, other(d)) for d in chips]
    both_ways = [(2 * d, 2 * d + 1) for d in chips] + [(2 * d + 1, 2 * d) for d in chips]
    return dict(
        core=lambda value: lax.ppermute(value, AXES, both_ways),
        across=move(swap, 0, 0),
        tiles=move(swap, 1, 1),
        before=move([(d + 1, d) for d in chips[:-1]], 0, 0),
        after=move([(d, d + 1) for d in chips[:-1]], 0, 0),
        ends=move([(half - 1, 0), (half, n_bins - 1)], 0, 0),
        beside=move([(d, d ^ plane) for d in chips], 0, 0),
        plane_sum=plane_sum,
    )


BLOCKS = [(0, 0), (0, 1), (0, 2), (0, 3), (1, 1), (1, 2), (1, 3), (1, 0)]
SENT = (1, 3, 3, 1)


def pack_kernel(held_ref, *refs):
    out_refs, (dv_ref, near_buf, far_buf, in_sem, out_sem) = refs[: len(SENT)], refs[len(SENT) :]
    rows, cols = iotas()
    count = len(BLOCKS)
    targets = [ref.at[pl.ds(j * LANE, LANE), :] for ref, blocks in zip(out_refs, SENT) for j in range(blocks)]

    def source(t, b, start, width):
        return held_ref.at[t, 0, pl.ds(b * LANE, LANE), pl.ds(start * LANE, width * LANE)]

    def near(n, start, width):
        return near_buf.at[n, :, pl.ds(start * LANE, width * LANE)]

    loads = [[] for _ in BLOCKS]
    for n, (t, k) in enumerate(BLOCKS):
        loads[n].append(pltpu.make_async_copy(source(t, 7 - k, 7 - k, 1), far_buf.at[n], in_sem.at[n]))
        loads[n].append(pltpu.make_async_copy(source(t, k, k, 8 - k), near(n, k, 8 - k), in_sem.at[count + n]))
        if k:
            loads[n].append(pltpu.make_async_copy(source(t, 7 - k, 8 - k, k), near(n, 0, k), in_sem.at[2 * count + n]))
        for copy in loads[n]:
            copy.start()
    stores = []
    for n, (t, k) in enumerate(BLOCKS):
        for copy in loads[n]:
            copy.wait()
        far = far_buf[n]
        block = near(n, k, 1)
        block[...] = jnp.where(cols >= rows, block[...], far.T)
        dv_ref[n] = jnp.sum(jnp.where(cols == rows, far, 0.0), axis=0, keepdims=True)
        stores.append(pltpu.make_async_copy(near_buf.at[n], targets[n], out_sem.at[n]))
        stores[-1].start()
    for copy in stores:
        copy.wait()


def pack(held):
    return pl.pallas_call(
        pack_kernel,
        in_specs=[pl.BlockSpec(memory_space=pl.ANY)],
        out_specs=[pl.BlockSpec(memory_space=pltpu.HBM)] * len(SENT) + [pl.BlockSpec(memory_space=pltpu.VMEM)],
        out_shape=[jax.ShapeDtypeStruct((blocks * LANE, 1024), F32) for blocks in SENT]
        + [jax.ShapeDtypeStruct((8, 1, LANE), F32)],
        scratch_shapes=[
            pltpu.VMEM((8, LANE, 1024), F32),
            pltpu.VMEM((8, LANE, LANE), F32),
            pltpu.SemaphoreType.DMA((24,)),
            pltpu.SemaphoreType.DMA((8,)),
        ],
        compiler_params=pltpu.CompilerParams(vmem_limit_bytes=VMEM_LIMIT),
        cost_estimate=pl.CostEstimate(flops=1 << 20, bytes_accessed=8 << 20, transcendentals=0),
        name="pack_triangles",
    )(held)


STREAMS = 4
ROWS = STREAMS * LANE


def sums_kernel(sc_ref, *refs):
    x_refs, (a_ref, b_ref, row_ref, col_ref, acc_ref) = refs[:STREAMS], refs[STREAMS:]
    i = pl.program_id(1)
    rows, cols = iotas()
    ahead = cols - rows

    @pl.when(i == 0)
    def _():
        acc_ref[...] = jnp.zeros_like(acc_ref)

    def add_up(masked):
        for r in range(STREAMS):
            a_line = a_ref[0, :, lanes(r)]
            a_col = as_column(a_line)
            start = i * ROWS + r * LANE
            across = jnp.zeros((LANE, LANE), F32)
            for k in range(8):
                x = x_refs[r][0, 0, :, lanes(k)]
                right = down = x
                if masked:
                    shift = start - k * LANE
                    right, down = jnp.where(ahead >= shift, x, 0.0), jnp.where(ahead > shift, x, 0.0)
                across += right * b_ref[0, :, lanes(k)]
                acc_ref[:, lanes(k)] += jnp.sum((down * a_col).reshape(LANE // 8, 8, LANE), axis=0)
            row_ref[0, :, lanes(r)] = jnp.sum(across.T, axis=0, keepdims=True) * a_line

    @pl.when(sc_ref[0] == 1)
    def _():
        add_up(True)

    @pl.when(sc_ref[0] == 0)
    def _():
        add_up(False)

    @pl.when(i == pl.num_programs(1) - 1)
    def _():
        col_ref[0] = jnp.sum(acc_ref[...], axis=0, keepdims=True) * b_ref[0]


def weighted_sums(scalars, held, row_w, col_w):
    steps = 1024 // ROWS
    shape = jax.ShapeDtypeStruct((2, 1, 1024), F32)

    def stream(r):
        return pl.BlockSpec((1, 1, LANE, 1024), lambda t, i, sc: (t, 0, STREAMS * i + r, 0))

    row_part, col_part = pl.pallas_call(
        sums_kernel,
        grid_spec=pltpu.PrefetchScalarGridSpec(
            num_scalar_prefetch=1,
            grid=(2, steps),
            in_specs=[stream(r) for r in range(STREAMS)]
            + [
                pl.BlockSpec((1, 1, ROWS), lambda t, i, sc: (t, 0, i)),
                pl.BlockSpec((1, 1, 1024), lambda t, i, sc: (t, 0, 0)),
            ],
            out_specs=[
                pl.BlockSpec((1, 1, ROWS), lambda t, i, sc: (t, 0, i)),
                pl.BlockSpec((1, 1, 1024), lambda t, i, sc: (t, 0, 0)),
            ],
            scratch_shapes=[pltpu.VMEM((8, 1024), F32)],
        ),
        out_shape=[shape, shape],
        compiler_params=pltpu.CompilerParams(vmem_limit_bytes=VMEM_LIMIT),
        cost_estimate=pl.CostEstimate(flops=8 << 20, bytes_accessed=8 << 20, transcendentals=0),
        name="weighted_sums",
    )(scalars, *[held] * STREAMS, row_w.reshape(2, 1, 1024), col_w.reshape(2, 1, 1024))
    return row_part.reshape(2, 1024), col_part.reshape(2, 1024)


def ahead_place(i):
    return 0, 0, jnp.where(i == 0, 0, 7)


def first_place(i):
    k = i // 2 + 1
    return 0, k, jnp.where(i % 2 == 0, k, 7 - k)


def mid_place(i):
    k = i // 2 + 1
    return 1, k, jnp.where(i % 2 == 0, k, 7 - k)


def last_place(i):
    return 1, 0, jnp.where(i == 0, 0, 7)


def balance_kernel(place, sc_ref, got_ref, held_ref, pk_ref, dv_ref, wr_ref, wc_ref, *rest):
    out_ref = rest[-1]
    t, k_now, b = place(pl.program_id(0))
    rows, cols = iotas()
    on_diagonal = sc_ref[0] == 1
    moved = sc_ref[1 + t] == 1
    w_col = as_column(wr_ref[0])

    def put(j, x):
        out_ref[0, 0, :, lanes(j)] = x * w_col * wc_ref[0, :, lanes(j)]

    @pl.when(moved & jnp.logical_not(on_diagonal))
    def _():
        for j in range(8):
            put(j, got_ref[0, 0, :, lanes(j)])

    @pl.when(jnp.logical_not(moved))
    def _():
        least = jnp.where(on_diagonal, 0, -4096) + b * LANE
        for j in range(8):
            put(j, jnp.where(cols - rows >= least - j * LANE, held_ref[0, 0, :, lanes(j)], 0.0))

    for k in range(4):
        @pl.when(moved & on_diagonal & (k_now == k) & (b == k))
        def _():
            for j in range(k):
                out_ref[0, 0, :, lanes(j)] = jnp.zeros((LANE, LANE), F32)
            put(k, jnp.where(cols >= rows, pk_ref[:, lanes(k)], 0.0))
            for j in range(k + 1, 8):
                put(j, pk_ref[:, lanes(j)])

        @pl.when(moved & on_diagonal & (k_now == k) & (b == 7 - k))
        def _():
            for j in range(7 - k):
                out_ref[0, 0, :, lanes(j)] = jnp.zeros((LANE, LANE), F32)
            far = pk_ref[:, lanes(k)].T
            put(7 - k, jnp.where(cols > rows, far, jnp.where(cols == rows, dv_ref[0], 0.0)))
            for j in range(k):
                put(8 - k + j, pk_ref[:, lanes(j)])


def balance(name, place, steps, first_k, scalars, got, held, packed, dv, wr, wc, into=None):
    tile = (1, 1, LANE, 1024)

    def got_at(i, sc):
        t, _, b = place(i)
        use = (sc[0] == 0) & (sc[1 + t] == 1)
        return (jnp.where(use, t, 0), 0, jnp.where(use, b, 0), 0)

    def held_at(i, sc):
        t, _, b = place(i)
        use = sc[1 + t] == 0
        return (jnp.where(use, t, 0), 0, jnp.where(use, b, 0), 0)

    def packed_at(i, sc):
        t, k, _ = place(i)
        use = (sc[0] == 1) & (sc[1 + t] == 1)
        return (jnp.where(use, k - first_k, 0), 0)

    def dv_at(i, sc):
        t, k, _ = place(i)
        return (k if t == 0 else jnp.where(k == 0, 7, 3 + k), 0, 0)

    in_specs = [
        pl.BlockSpec(tile, got_at),
        pl.BlockSpec(tile, held_at),
        pl.BlockSpec((LANE, 1024), packed_at),
        pl.BlockSpec((1, 1, LANE), dv_at),
        pl.BlockSpec((1, 1, LANE), lambda i, sc: (place(i)[0] * 8 + place(i)[2], 0, 0)),
        pl.BlockSpec((1, 1, 1024), lambda i, sc: (place(i)[0], 0, 0)),
    ]
    args = [scalars, got, held, packed, dv, wr, wc]
    aliases = {}
    if into is not None:
        in_specs.append(pl.BlockSpec(memory_space=pl.ANY))
        args.append(into)
        aliases = {len(args) - 1: 0}
    return pl.pallas_call(
        functools.partial(balance_kernel, place),
        grid_spec=pltpu.PrefetchScalarGridSpec(
            num_scalar_prefetch=1,
            grid=(steps,),
            in_specs=in_specs,
            out_specs=pl.BlockSpec(tile, lambda i, sc: (place(i)[0], 0, place(i)[2], 0)),
        ),
        out_shape=jax.ShapeDtypeStruct(held.shape, F32),
        input_output_aliases=aliases,
        compiler_params=pltpu.CompilerParams(vmem_limit_bytes=VMEM_LIMIT),
        cost_estimate=pl.CostEstimate(flops=steps << 18, bytes_accessed=steps << 20, transcendentals=0),
        name=name,
    )(*args)


def local(held_tiles, placed, bin_mask, bias):
    move = moves(lax.axis_size("bins"))
    on_diagonal = lax.axis_index("diag") == 0
    live = bin_mask.astype(F32).reshape(2, 1024)
    scalars = jnp.concatenate([on_diagonal.astype(jnp.int32)[None], (placed == 1).astype(jnp.int32)])

    got = move["tiles"](held_tiles)
    ahead, first, mid, last, dv = pack(held_tiles)

    here = lax.axis_index("bins")
    there = here ^ (lax.axis_size("bins") // 2)
    moved = placed[1] == 1

    def stored(lines):
        row_lines = [lines[3:4], jnp.where(moved, lines[4:5], lines[1:2])]
        next_lines = [lines[4:5], jnp.where(moved, lines[5:6], lines[2:3])]
        return jnp.concatenate(row_lines, axis=0), jnp.concatenate(next_lines, axis=0)

    def stored_parts(lines):
        rows, following = stored(lines)
        passed = move["core"](jnp.concatenate([rows, following], axis=0))
        row_w, col_w = jnp.where(on_diagonal, rows, passed[:2]), jnp.where(on_diagonal, rows, passed[2:])
        row_part, col_part = weighted_sums(scalars, held_tiles, row_w, col_w)
        off = move["core"](jnp.concatenate([row_part, col_part], axis=0))
        return row_part + col_part + off[:2], off[2:]

    def home_sums(mine, theirs):
        rows_d = [theirs[0:1], jnp.where(moved, theirs[1:2], mine[1:2])]
        rows_p = [mine[0:1], jnp.where(moved, mine[1:2], theirs[1:2])]
        cols_d = [theirs[2:3], jnp.where(moved, theirs[3:4], mine[3:4])]
        cols_p = [mine[2:3], jnp.where(moved, mine[3:4], theirs[3:4])]
        return rows_d, rows_p, cols_d, cols_p

    def sums_of(parts, which, cols_before, rows_after):
        rows, cols = parts[which], parts[2 + which]
        first = (there if which else here) == 0
        return jnp.concatenate(
            [rows[0] + jnp.where(first, 0.0, cols_before), rows[1] + cols[0], rows_after + cols[1]], axis=0
        )

    def neighbours(parts, count):
        rows_d, rows_p, cols_d, cols_p = parts
        cols_before = move["after"](jnp.concatenate([cols_d[1], cols_p[1]][:count], axis=0))
        rows_after = move["before"](jnp.concatenate([rows_d[0], rows_p[0]][:count], axis=0))
        return cols_before, rows_after

    after_live = move["before"](live[:1])
    live_lines = jnp.concatenate([live, after_live], axis=0)
    live_lines = jnp.concatenate([live_lines, move["across"](live_lines)], axis=0)

    rows, cols = stored_parts(live_lines)
    line_1 = rows[:1] + rows[1:] + cols[:1] + cols[1:]
    mine = jnp.concatenate([rows, cols], axis=0)
    parts = home_sums(mine, move["across"](mine))
    ends = move["ends"](jnp.concatenate([parts[2][1], parts[0][0]], axis=0))
    ends, cols_before, rows_after, ahead = lax.optimization_barrier((ends, *neighbours(parts, 2), ahead))
    ahead = move["across"](ahead)
    cols_before = [cols_before[0:1], jnp.where(here == 0, ends[0:1], cols_before[1:2])]
    rows_after = [rows_after[0:1], jnp.where(there == lax.axis_size("bins") // 2 - 1, ends[1:2], rows_after[1:2])]
    sums_1 = jnp.concatenate([sums_of(parts, 0, cols_before[0], rows_after[0]), sums_of(parts, 1, cols_before[1], rows_after[1])], axis=0)

    rows, cols = stored_parts(jnp.where(live_lines > 0, 1.0 / sums_1, 0.0))
    rows, cols, ahead = lax.optimization_barrier((rows, cols, ahead))
    totals = [line_1, rows[:1] + rows[1:] + cols[:1] + cols[1:], live[:1] + live[1:]]
    mine = jnp.concatenate([rows, cols, *totals, dv.reshape(1, 1024)], axis=0)
    theirs = move["across"](mine)
    parts = home_sums(mine, theirs)
    dv = theirs[7:8].reshape(8, 1, LANE)
    totals = jnp.sum((mine[4:7] + theirs[4:7]).reshape(3, 8, LANE), axis=1).reshape(1, 3 * LANE)
    beside, *around, first, mid, last = lax.optimization_barrier(
        (move["beside"](totals), *neighbours(parts, 1), first, mid, last)
    )
    first, mid, last = move["across"](first), move["across"](mid), move["across"](last)
    totals = move["plane_sum"](totals + beside)
    sums_2 = sums_of(parts, 0, *around)
    totals = jnp.sum(totals.reshape(3, LANE), axis=1)
    scale = (totals[0] / totals[2]) * (totals[1] / totals[2])

    products = sums_1[:3] * sums_2
    weights = jnp.where(live_lines[:3] > 0, scale / products, 0.0)
    factor = jnp.where(live > 0, products[:2] / scale, 1.0)
    result = jnp.concatenate([weights, factor], axis=0)
    result = jnp.where(on_diagonal, result, move["core"](result))
    bias_out = bias.reshape(2, 1024) * result[3:]
    wr = result[:2].reshape(16, 1, LANE)
    wc = jnp.where(on_diagonal, result[:2], result[1:3]).reshape(2, 1, 1024)

    got, ahead, wr, wc, dv = lax.optimization_barrier((got, ahead, wr, wc, dv))
    out = balance("balance_ahead", ahead_place, 2, 0, scalars, got, held_tiles, ahead, dv, wr, wc)
    out, first = lax.optimization_barrier((out, first))
    out = balance("balance_first", first_place, 6, 1, scalars, got, held_tiles, first, dv, wr, wc, into=out)
    out, mid = lax.optimization_barrier((out, mid))
    out = balance("balance_mid", mid_place, 6, 1, scalars, got, held_tiles, mid, dv, wr, wc, into=out)
    out, last = lax.optimization_barrier((out, last))
    out = balance("balance_last", last_place, 2, 0, scalars, got, held_tiles, last, dv, wr, wc, into=out)
    return out, bias_out.reshape(2048)


def solution(mesh):
    placed = (P("bins", "diag", None, None), P("bins"), P("bins"), P("bins"))
    return jax.shard_map(
        local,
        mesh=mesh,
        in_specs=placed,
        out_specs=(P("bins", "diag", None, None), P("bins")),
        check_vma=False,
    )
```

```python
import functools

import jax
import jax.numpy as jnp
from jax import lax
from jax.experimental import pallas as pl
from jax.experimental.pallas import tpu as pltpu
from jax.sharding import PartitionSpec as P

AXES = ("bins", "diag")
F32 = jnp.float32
LANE = 128
VMEM_LIMIT = 48 * 1024 * 1024


def iotas():
    rows = lax.broadcasted_iota(jnp.int32, (LANE, LANE), 0)
    cols = lax.broadcasted_iota(jnp.int32, (LANE, LANE), 1)
    return rows, cols


def as_column(line):
    return jnp.broadcast_to(line, (LANE, LANE)).T


def lanes(k):
    return pl.ds(k * LANE, LANE)


def moves(n_bins):
    half = n_bins // 2
    chips = range(n_bins)

    def other(d):
        return (d + half) % n_bins

    def move(pairs, source_core, target_core):
        pairs = [(2 * s + source_core, 2 * t + target_core) for s, t in pairs]
        return lambda value: lax.ppermute(value, AXES, pairs)

    plane = max(n_bins // 4, 1)
    planes = [list(range(start, start + plane)) for start in range(0, n_bins, plane)]

    def plane_sum(value):
        spread = jnp.broadcast_to(value, (plane, value.shape[1]))
        seen = lax.all_to_all(spread, "bins", 0, 0, axis_index_groups=planes, tiled=True)
        return jnp.sum(seen, axis=0, keepdims=True)

    same = [(d, d) for d in chips]
    swap = [(d, other(d)) for d in chips]
    both_ways = [(2 * d, 2 * d + 1) for d in chips] + [(2 * d + 1, 2 * d) for d in chips]
    return dict(
        core=lambda value: lax.ppermute(value, AXES, both_ways),
        across=move(swap, 0, 0),
        tiles=move(swap, 1, 1),
        before=move([(d + 1, d) for d in chips[:-1]], 0, 0),
        after=move([(d, d + 1) for d in chips[:-1]], 0, 0),
        ends=move([(half - 1, 0), (half, n_bins - 1)], 0, 0),
        beside=move([(d, d ^ plane) for d in chips], 0, 0),
        plane_sum=plane_sum,
    )


BLOCKS = [(0, 0), (0, 1), (0, 2), (0, 3), (1, 1), (1, 2), (1, 3), (1, 0)]
SENT = (3, 4, 1)


def pack_kernel(held_ref, *refs):
    out_refs, (dv_ref, near_buf, far_buf, in_sem, out_sem) = refs[: len(SENT)], refs[len(SENT) :]
    rows, cols = iotas()
    count = len(BLOCKS)
    targets = [ref.at[pl.ds(j * LANE, LANE), :] for ref, blocks in zip(out_refs, SENT) for j in range(blocks)]

    def source(t, b, start, width):
        return held_ref.at[t, 0, pl.ds(b * LANE, LANE), pl.ds(start * LANE, width * LANE)]

    def near(n, start, width):
        return near_buf.at[n, :, pl.ds(start * LANE, width * LANE)]

    loads = [[] for _ in BLOCKS]
    for n, (t, k) in enumerate(BLOCKS):
        loads[n].append(pltpu.make_async_copy(source(t, 7 - k, 7 - k, 1), far_buf.at[n], in_sem.at[n]))
        loads[n].append(pltpu.make_async_copy(source(t, k, k, 8 - k), near(n, k, 8 - k), in_sem.at[count + n]))
        if k:
            loads[n].append(pltpu.make_async_copy(source(t, 7 - k, 8 - k, k), near(n, 0, k), in_sem.at[2 * count + n]))
        for copy in loads[n]:
            copy.start()
    stores = []
    for n, (t, k) in enumerate(BLOCKS):
        for copy in loads[n]:
            copy.wait()
        far = far_buf[n]
        block = near(n, k, 1)
        block[...] = jnp.where(cols >= rows, block[...], far.T)
        dv_ref[n] = jnp.sum(jnp.where(cols == rows, far, 0.0), axis=0, keepdims=True)
        stores.append(pltpu.make_async_copy(near_buf.at[n], targets[n], out_sem.at[n]))
        stores[-1].start()
    for copy in stores:
        copy.wait()


def pack(held):
    return pl.pallas_call(
        pack_kernel,
        in_specs=[pl.BlockSpec(memory_space=pl.ANY)],
        out_specs=[pl.BlockSpec(memory_space=pltpu.HBM)] * len(SENT) + [pl.BlockSpec(memory_space=pltpu.VMEM)],
        out_shape=[jax.ShapeDtypeStruct((blocks * LANE, 1024), F32) for blocks in SENT]
        + [jax.ShapeDtypeStruct((8, 1, LANE), F32)],
        scratch_shapes=[
            pltpu.VMEM((8, LANE, 1024), F32),
            pltpu.VMEM((8, LANE, LANE), F32),
            pltpu.SemaphoreType.DMA((24,)),
            pltpu.SemaphoreType.DMA((8,)),
        ],
        compiler_params=pltpu.CompilerParams(vmem_limit_bytes=VMEM_LIMIT),
        cost_estimate=pl.CostEstimate(flops=1 << 20, bytes_accessed=8 << 20, transcendentals=0),
        name="pack_triangles",
    )(held)


def sums_kernel(sc_ref, held_ref, a_ref, b_ref, row_ref, col_ref, buf, sem):
    rows, cols = iotas()

    def add_up(triangle):
        copies = []
        for n in range(16):
            t, b = n // 8, n % 8
            near = pl.ds(b * LANE, LANE)
            kept = pl.ds(b * LANE, (8 - b) * LANE) if triangle else pl.ds(0, 1024)
            copies.append(pltpu.make_async_copy(held_ref.at[t, 0, near, kept], buf.at[t, near, kept], sem.at[n]))
            copies[-1].start()
        for t in range(2):
            below = [jnp.zeros((8, LANE), F32) for _ in range(8)]
            for b in range(8):
                copies[8 * t + b].wait()
                a_line = a_ref[t, :, lanes(b)]
                a_col = as_column(a_line)
                across = jnp.zeros((LANE, LANE), F32)
                for k in range(b if triangle else 0, 8):
                    right = down = buf[t, pl.ds(b * LANE, LANE), lanes(k)]
                    if triangle and k == b:
                        right, down = jnp.where(cols >= rows, right, 0.0), jnp.where(cols > rows, down, 0.0)
                    across += right * b_ref[t, :, lanes(k)]
                    below[k] += jnp.sum((down * a_col).reshape(LANE // 8, 8, LANE), axis=0)
                row_ref[t, :, lanes(b)] = jnp.sum(across.T, axis=0, keepdims=True) * a_line
            for k in range(8):
                col_ref[t, :, lanes(k)] = jnp.sum(below[k], axis=0, keepdims=True) * b_ref[t, :, lanes(k)]

    @pl.when(sc_ref[0] == 1)
    def _():
        add_up(True)

    @pl.when(sc_ref[0] == 0)
    def _():
        add_up(False)


def weighted_sums(scalars, held, row_w, col_w):
    shape = jax.ShapeDtypeStruct((2, 1, 1024), F32)
    here = pl.BlockSpec(memory_space=pltpu.VMEM)
    row_part, col_part = pl.pallas_call(
        sums_kernel,
        in_specs=[pl.BlockSpec(memory_space=pltpu.SMEM), pl.BlockSpec(memory_space=pl.ANY), here, here],
        out_specs=[here, here],
        out_shape=[shape, shape],
        scratch_shapes=[pltpu.VMEM((2, 1024, 1024), F32), pltpu.SemaphoreType.DMA((16,))],
        compiler_params=pltpu.CompilerParams(vmem_limit_bytes=VMEM_LIMIT),
        cost_estimate=pl.CostEstimate(flops=8 << 20, bytes_accessed=8 << 20, transcendentals=0),
        name="weighted_sums",
    )(scalars, held, row_w.reshape(2, 1, 1024), col_w.reshape(2, 1, 1024))
    return row_part.reshape(2, 1024), col_part.reshape(2, 1024)


def balance_kernel(t, ks, base, sc_ref, got_ref, held_ref, pk_ref, dv_ref, wr_ref, wc_ref, *rest):
    out_ref, buf, pk_buf, in_sem, out_sem = rest[-5:]
    rows, cols = iotas()
    on_diagonal = sc_ref[0] == 1
    moved = sc_ref[1 + t] == 1
    blocks = [b for k in ks for b in (k, 7 - k)]

    def place(ref, b):
        return ref.at[t, 0, pl.ds(b * LANE, LANE), :]

    def put(i, b, w_col, j, x):
        buf[i, :, lanes(j)] = x * w_col * wc_ref[t, :, lanes(j)]

    def send(i, b):
        copy = pltpu.make_async_copy(buf.at[i], place(out_ref, b), out_sem.at[i])
        copy.start()
        return copy

    def from_rows(ref, masked):
        loads = [pltpu.make_async_copy(place(ref, b), buf.at[i], in_sem.at[i]) for i, b in enumerate(blocks)]
        for copy in loads:
            copy.start()
        stores = []
        for i, b in enumerate(blocks):
            loads[i].wait()
            w_col = as_column(wr_ref[t * 8 + b])
            for j in range(8):
                x = buf[i, :, lanes(j)]
                put(i, b, w_col, j, jnp.where(cols - rows >= (b - j) * LANE, x, 0.0) if masked else x)
            stores.append(send(i, b))
        for copy in stores:
            copy.wait()

    @pl.when(moved & jnp.logical_not(on_diagonal))
    def _():
        from_rows(got_ref, False)

    @pl.when(jnp.logical_not(moved) & jnp.logical_not(on_diagonal))
    def _():
        from_rows(held_ref, False)

    @pl.when(jnp.logical_not(moved) & on_diagonal)
    def _():
        from_rows(held_ref, True)

    @pl.when(moved & on_diagonal)
    def _():
        loads = [
            pltpu.make_async_copy(pk_ref.at[pl.ds((base + n) * LANE, LANE), :], pk_buf.at[n], in_sem.at[n])
            for n in range(len(ks))
        ]
        for copy in loads:
            copy.start()
        stores = []
        for n, k in enumerate(ks):
            loads[n].wait()
            near, far = 2 * n, 2 * n + 1
            w_col = as_column(wr_ref[t * 8 + k])
            for j in range(k):
                buf[near, :, lanes(j)] = jnp.zeros((LANE, LANE), F32)
            put(near, k, w_col, k, jnp.where(cols >= rows, pk_buf[n, :, lanes(k)], 0.0))
            for j in range(k + 1, 8):
                put(near, k, w_col, j, pk_buf[n, :, lanes(j)])
            stores.append(send(near, k))
            w_col = as_column(wr_ref[t * 8 + 7 - k])
            for j in range(7 - k):
                buf[far, :, lanes(j)] = jnp.zeros((LANE, LANE), F32)
            diagonal = dv_ref[BLOCKS.index((t, k))]
            block = jnp.where(cols > rows, pk_buf[n, :, lanes(k)].T, jnp.where(cols == rows, diagonal, 0.0))
            put(far, 7 - k, w_col, 7 - k, block)
            for j in range(k):
                put(far, 7 - k, w_col, 8 - k + j, pk_buf[n, :, lanes(j)])
            stores.append(send(far, 7 - k))
        for copy in stores:
            copy.wait()


def balance(name, t, ks, scalars, got, held, packed, dv, wr, wc, into=None, base=0):
    here, anywhere = pl.BlockSpec(memory_space=pltpu.VMEM), pl.BlockSpec(memory_space=pl.ANY)
    args = [scalars, got, held, packed, dv, wr, wc]
    in_specs = [pl.BlockSpec(memory_space=pltpu.SMEM), anywhere, anywhere, anywhere, here, here, here]
    aliases = {}
    if into is not None:
        aliases = {len(args): 0}
        in_specs.append(anywhere)
        args.append(into)
    count = 2 * len(ks)
    return pl.pallas_call(
        functools.partial(balance_kernel, t, ks, base),
        in_specs=in_specs,
        out_specs=anywhere,
        out_shape=jax.ShapeDtypeStruct(held.shape, F32),
        scratch_shapes=[
            pltpu.VMEM((count, LANE, 1024), F32),
            pltpu.VMEM((len(ks), LANE, 1024), F32),
            pltpu.SemaphoreType.DMA((count,)),
            pltpu.SemaphoreType.DMA((count,)),
        ],
        input_output_aliases=aliases,
        compiler_params=pltpu.CompilerParams(vmem_limit_bytes=VMEM_LIMIT),
        cost_estimate=pl.CostEstimate(flops=count << 18, bytes_accessed=count << 20, transcendentals=0),
        name=name,
    )(*args)


def local(held_tiles, placed, bin_mask, bias):
    move = moves(lax.axis_size("bins"))
    on_diagonal = lax.axis_index("diag") == 0
    live = bin_mask.astype(F32).reshape(2, 1024)
    scalars = jnp.concatenate([on_diagonal.astype(jnp.int32)[None], (placed == 1).astype(jnp.int32)])

    got = move["tiles"](held_tiles)
    ahead, most, last, dv = pack(held_tiles)

    here = lax.axis_index("bins")
    there = here ^ (lax.axis_size("bins") // 2)
    moved = placed[1] == 1

    def stored(lines):
        row_lines = [lines[3:4], jnp.where(moved, lines[4:5], lines[1:2])]
        next_lines = [lines[4:5], jnp.where(moved, lines[5:6], lines[2:3])]
        return jnp.concatenate(row_lines, axis=0), jnp.concatenate(next_lines, axis=0)

    def stored_parts(lines):
        rows, following = stored(lines)
        passed = move["core"](jnp.concatenate([rows, following], axis=0))
        row_w, col_w = jnp.where(on_diagonal, rows, passed[:2]), jnp.where(on_diagonal, rows, passed[2:])
        row_part, col_part = weighted_sums(scalars, held_tiles, row_w, col_w)
        off = move["core"](jnp.concatenate([row_part, col_part], axis=0))
        return row_part + col_part + off[:2], off[2:]

    def home_sums(mine, theirs):
        rows_d = [theirs[0:1], jnp.where(moved, theirs[1:2], mine[1:2])]
        rows_p = [mine[0:1], jnp.where(moved, mine[1:2], theirs[1:2])]
        cols_d = [theirs[2:3], jnp.where(moved, theirs[3:4], mine[3:4])]
        cols_p = [mine[2:3], jnp.where(moved, mine[3:4], theirs[3:4])]
        return rows_d, rows_p, cols_d, cols_p

    def sums_of(parts, which, cols_before, rows_after):
        rows, cols = parts[which], parts[2 + which]
        first = (there if which else here) == 0
        return jnp.concatenate(
            [rows[0] + jnp.where(first, 0.0, cols_before), rows[1] + cols[0], rows_after + cols[1]], axis=0
        )

    def neighbours(parts, count):
        rows_d, rows_p, cols_d, cols_p = parts
        cols_before = move["after"](jnp.concatenate([cols_d[1], cols_p[1]][:count], axis=0))
        rows_after = move["before"](jnp.concatenate([rows_d[0], rows_p[0]][:count], axis=0))
        return cols_before, rows_after

    after_live = move["before"](live[:1])
    live_lines = jnp.concatenate([live, after_live], axis=0)
    live_lines = jnp.concatenate([live_lines, move["across"](live_lines)], axis=0)
    live_lines, ahead = lax.optimization_barrier((live_lines, ahead))
    ahead = move["across"](ahead)

    rows, cols = stored_parts(live_lines)
    rows, cols, ahead = lax.optimization_barrier((rows, cols, ahead))
    line_1 = rows[:1] + rows[1:] + cols[:1] + cols[1:]
    mine = jnp.concatenate([rows, cols], axis=0)
    parts = home_sums(mine, move["across"](mine))
    ends = move["ends"](jnp.concatenate([parts[2][1], parts[0][0]], axis=0))
    ends, cols_before, rows_after = lax.optimization_barrier((ends, *neighbours(parts, 2)))
    cols_before = [cols_before[0:1], jnp.where(here == 0, ends[0:1], cols_before[1:2])]
    rows_after = [rows_after[0:1], jnp.where(there == lax.axis_size("bins") // 2 - 1, ends[1:2], rows_after[1:2])]
    sums_1 = jnp.concatenate([sums_of(parts, 0, cols_before[0], rows_after[0]), sums_of(parts, 1, cols_before[1], rows_after[1])], axis=0)

    rows, cols = stored_parts(jnp.where(live_lines > 0, 1.0 / sums_1, 0.0))
    totals = [line_1, rows[:1] + rows[1:] + cols[:1] + cols[1:], live[:1] + live[1:]]
    mine = jnp.concatenate([rows, cols, *totals, dv.reshape(1, 1024)], axis=0)
    theirs = move["across"](mine)
    parts = home_sums(mine, theirs)
    dv = theirs[7:8].reshape(8, 1, LANE)
    totals = jnp.sum((mine[4:7] + theirs[4:7]).reshape(3, 8, LANE), axis=1).reshape(1, 3 * LANE)
    beside, *around, most, last = lax.optimization_barrier(
        (move["beside"](totals), *neighbours(parts, 1), most, last)
    )
    most, last = move["across"](most), move["across"](last)
    totals = move["plane_sum"](totals + beside)
    sums_2 = sums_of(parts, 0, *around)
    totals = jnp.sum(totals.reshape(3, LANE), axis=1)
    scale = (totals[0] / totals[2]) * (totals[1] / totals[2])

    products = sums_1[:3] * sums_2
    weights = jnp.where(live_lines[:3] > 0, scale / products, 0.0)
    factor = jnp.where(live > 0, products[:2] / scale, 1.0)
    result = jnp.concatenate([weights, factor], axis=0)
    result = jnp.where(on_diagonal, result, move["core"](result))
    bias_out = bias.reshape(2, 1024) * result[3:]
    wr = result[:2].reshape(16, 1, LANE)
    wc = jnp.where(on_diagonal, result[:2], result[1:3]).reshape(2, 1, 1024)

    got, ahead, wr, wc, dv = lax.optimization_barrier((got, ahead, wr, wc, dv))
    out = balance("balance_ahead", 0, (0, 1, 2), scalars, got, held_tiles, ahead, dv, wr, wc)
    out, most = lax.optimization_barrier((out, most))
    out = balance("balance_most", 0, (3,), scalars, got, held_tiles, most, dv, wr, wc, into=out)
    out = balance("balance_rest", 1, (1, 2, 3), scalars, got, held_tiles, most, dv, wr, wc, into=out, base=1)
    out, last = lax.optimization_barrier((out, last))
    out = balance("balance_last", 1, (0,), scalars, got, held_tiles, last, dv, wr, wc, into=out)
    return out, bias_out.reshape(2048)


def solution(mesh):
    placed = (P("bins", "diag", None, None), P("bins"), P("bins"), P("bins"))
    return jax.shard_map(
        local,
        mesh=mesh,
        in_specs=placed,
        out_specs=(P("bins", "diag", None, None), P("bins")),
        check_vma=False,
    )
```

```python
import functools

import jax
import jax.numpy as jnp
from jax import lax
from jax.experimental import pallas as pl
from jax.experimental.pallas import tpu as pltpu
from jax.sharding import PartitionSpec as P

AXES = ("bins", "diag")
F32 = jnp.float32
LANE = 128
VMEM_LIMIT = 48 * 1024 * 1024


def iotas():
    rows = lax.broadcasted_iota(jnp.int32, (LANE, LANE), 0)
    cols = lax.broadcasted_iota(jnp.int32, (LANE, LANE), 1)
    return rows, cols


def as_column(line):
    return jnp.broadcast_to(line, (LANE, LANE)).T


def lanes(k):
    return pl.ds(k * LANE, LANE)


def moves(n_bins):
    half = n_bins // 2
    chips = range(n_bins)

    def other(d):
        return (d + half) % n_bins

    def move(pairs, source_core, target_core):
        pairs = [(2 * s + source_core, 2 * t + target_core) for s, t in pairs]
        return lambda value: lax.ppermute(value, AXES, pairs)

    plane = max(n_bins // 4, 1)
    planes = [list(range(start, start + plane)) for start in range(0, n_bins, plane)]

    def plane_sum(value):
        spread = jnp.broadcast_to(value, (plane, value.shape[1]))
        seen = lax.all_to_all(spread, "bins", 0, 0, axis_index_groups=planes, tiled=True)
        return jnp.sum(seen, axis=0, keepdims=True)

    same = [(d, d) for d in chips]
    swap = [(d, other(d)) for d in chips]
    both_ways = [(2 * d, 2 * d + 1) for d in chips] + [(2 * d + 1, 2 * d) for d in chips]
    return dict(
        core=lambda value: lax.ppermute(value, AXES, both_ways),
        across=move(swap, 0, 0),
        tiles=move(swap, 1, 1),
        before=move([(d + 1, d) for d in chips[:-1]], 0, 0),
        after=move([(d, d + 1) for d in chips[:-1]], 0, 0),
        ends=move([(half - 1, 0), (half, n_bins - 1)], 0, 0),
        beside=move([(d, d ^ plane) for d in chips], 0, 0),
        plane_sum=plane_sum,
    )


BLOCKS = [(0, 0), (0, 1), (0, 2), (0, 3), (1, 1), (1, 2), (1, 3), (1, 0)]
SENT = (2, 5, 1)


def pack_kernel(held_ref, *refs):
    out_refs, (dv_ref, near_buf, far_buf, in_sem, out_sem) = refs[: len(SENT)], refs[len(SENT) :]
    rows, cols = iotas()
    count = len(BLOCKS)
    targets = [ref.at[pl.ds(j * LANE, LANE), :] for ref, blocks in zip(out_refs, SENT) for j in range(blocks)]

    def source(t, b, start, width):
        return held_ref.at[t, 0, pl.ds(b * LANE, LANE), pl.ds(start * LANE, width * LANE)]

    def near(n, start, width):
        return near_buf.at[n, :, pl.ds(start * LANE, width * LANE)]

    loads = [[] for _ in BLOCKS]
    for n, (t, k) in enumerate(BLOCKS):
        loads[n].append(pltpu.make_async_copy(source(t, 7 - k, 7 - k, 1), far_buf.at[n], in_sem.at[n]))
        loads[n].append(pltpu.make_async_copy(source(t, k, k, 8 - k), near(n, k, 8 - k), in_sem.at[count + n]))
        if k:
            loads[n].append(pltpu.make_async_copy(source(t, 7 - k, 8 - k, k), near(n, 0, k), in_sem.at[2 * count + n]))
        for copy in loads[n]:
            copy.start()
    stores = []
    for n, (t, k) in enumerate(BLOCKS):
        for copy in loads[n]:
            copy.wait()
        far = far_buf[n]
        block = near(n, k, 1)
        block[...] = jnp.where(cols >= rows, block[...], far.T)
        dv_ref[n] = jnp.sum(jnp.where(cols == rows, far, 0.0), axis=0, keepdims=True)
        stores.append(pltpu.make_async_copy(near_buf.at[n], targets[n], out_sem.at[n]))
        stores[-1].start()
    for copy in stores:
        copy.wait()


def pack(held):
    return pl.pallas_call(
        pack_kernel,
        in_specs=[pl.BlockSpec(memory_space=pl.ANY)],
        out_specs=[pl.BlockSpec(memory_space=pltpu.HBM)] * len(SENT) + [pl.BlockSpec(memory_space=pltpu.VMEM)],
        out_shape=[jax.ShapeDtypeStruct((blocks * LANE, 1024), F32) for blocks in SENT]
        + [jax.ShapeDtypeStruct((8, 1, LANE), F32)],
        scratch_shapes=[
            pltpu.VMEM((8, LANE, 1024), F32),
            pltpu.VMEM((8, LANE, LANE), F32),
            pltpu.SemaphoreType.DMA((24,)),
            pltpu.SemaphoreType.DMA((8,)),
        ],
        compiler_params=pltpu.CompilerParams(vmem_limit_bytes=VMEM_LIMIT),
        cost_estimate=pl.CostEstimate(flops=1 << 20, bytes_accessed=8 << 20, transcendentals=0),
        name="pack_triangles",
    )(held)


def sums_kernel(sc_ref, held_ref, a_ref, b_ref, row_ref, col_ref, buf, sem):
    rows, cols = iotas()

    def add_up(triangle):
        copies = []
        for n in range(16):
            t, b = n // 8, n % 8
            near = pl.ds(b * LANE, LANE)
            kept = pl.ds(b * LANE, (8 - b) * LANE) if triangle else pl.ds(0, 1024)
            copies.append(pltpu.make_async_copy(held_ref.at[t, 0, near, kept], buf.at[t, near, kept], sem.at[n]))
            copies[-1].start()
        for t in range(2):
            below = [jnp.zeros((8, LANE), F32) for _ in range(8)]
            for b in range(8):
                copies[8 * t + b].wait()
                a_line = a_ref[t, :, lanes(b)]
                a_col = as_column(a_line)
                across = jnp.zeros((LANE, LANE), F32)
                for k in range(b if triangle else 0, 8):
                    right = down = buf[t, pl.ds(b * LANE, LANE), lanes(k)]
                    if triangle and k == b:
                        right, down = jnp.where(cols >= rows, right, 0.0), jnp.where(cols > rows, down, 0.0)
                    across += right * b_ref[t, :, lanes(k)]
                    below[k] += jnp.sum((down * a_col).reshape(LANE // 8, 8, LANE), axis=0)
                row_ref[t, :, lanes(b)] = jnp.sum(across.T, axis=0, keepdims=True) * a_line
            for k in range(8):
                col_ref[t, :, lanes(k)] = jnp.sum(below[k], axis=0, keepdims=True) * b_ref[t, :, lanes(k)]

    @pl.when(sc_ref[0] == 1)
    def _():
        add_up(True)

    @pl.when(sc_ref[0] == 0)
    def _():
        add_up(False)


def weighted_sums(scalars, held, row_w, col_w):
    shape = jax.ShapeDtypeStruct((2, 1, 1024), F32)
    here = pl.BlockSpec(memory_space=pltpu.VMEM)
    row_part, col_part = pl.pallas_call(
        sums_kernel,
        in_specs=[pl.BlockSpec(memory_space=pltpu.SMEM), pl.BlockSpec(memory_space=pl.ANY), here, here],
        out_specs=[here, here],
        out_shape=[shape, shape],
        scratch_shapes=[pltpu.VMEM((2, 1024, 1024), F32), pltpu.SemaphoreType.DMA((16,))],
        compiler_params=pltpu.CompilerParams(vmem_limit_bytes=VMEM_LIMIT),
        cost_estimate=pl.CostEstimate(flops=8 << 20, bytes_accessed=8 << 20, transcendentals=0),
        name="weighted_sums",
    )(scalars, held, row_w.reshape(2, 1, 1024), col_w.reshape(2, 1, 1024))
    return row_part.reshape(2, 1024), col_part.reshape(2, 1024)


def balance_kernel(t, ks, base, sc_ref, got_ref, held_ref, pk_ref, dv_ref, wr_ref, wc_ref, *rest):
    out_ref, buf, pk_buf, in_sem, out_sem = rest[-5:]
    rows, cols = iotas()
    on_diagonal = sc_ref[0] == 1
    moved = sc_ref[1 + t] == 1
    blocks = [b for k in ks for b in (k, 7 - k)]

    def place(ref, b):
        return ref.at[t, 0, pl.ds(b * LANE, LANE), :]

    def put(i, b, w_col, j, x):
        buf[i, :, lanes(j)] = x * w_col * wc_ref[t, :, lanes(j)]

    def send(i, b):
        copy = pltpu.make_async_copy(buf.at[i], place(out_ref, b), out_sem.at[i])
        copy.start()
        return copy

    def from_rows(ref, masked):
        loads = [pltpu.make_async_copy(place(ref, b), buf.at[i], in_sem.at[i]) for i, b in enumerate(blocks)]
        for copy in loads:
            copy.start()
        stores = []
        for i, b in enumerate(blocks):
            loads[i].wait()
            w_col = as_column(wr_ref[t * 8 + b])
            for j in range(8):
                x = buf[i, :, lanes(j)]
                put(i, b, w_col, j, jnp.where(cols - rows >= (b - j) * LANE, x, 0.0) if masked else x)
            stores.append(send(i, b))
        for copy in stores:
            copy.wait()

    @pl.when(moved & jnp.logical_not(on_diagonal))
    def _():
        from_rows(got_ref, False)

    @pl.when(jnp.logical_not(moved) & jnp.logical_not(on_diagonal))
    def _():
        from_rows(held_ref, False)

    @pl.when(jnp.logical_not(moved) & on_diagonal)
    def _():
        from_rows(held_ref, True)

    @pl.when(moved & on_diagonal)
    def _():
        loads = [
            pltpu.make_async_copy(pk_ref.at[pl.ds((base + n) * LANE, LANE), :], pk_buf.at[n], in_sem.at[n])
            for n in range(len(ks))
        ]
        for copy in loads:
            copy.start()
        stores = []
        for n, k in enumerate(ks):
            loads[n].wait()
            near, far = 2 * n, 2 * n + 1
            w_col = as_column(wr_ref[t * 8 + k])
            for j in range(k):
                buf[near, :, lanes(j)] = jnp.zeros((LANE, LANE), F32)
            put(near, k, w_col, k, jnp.where(cols >= rows, pk_buf[n, :, lanes(k)], 0.0))
            for j in range(k + 1, 8):
                put(near, k, w_col, j, pk_buf[n, :, lanes(j)])
            stores.append(send(near, k))
            w_col = as_column(wr_ref[t * 8 + 7 - k])
            for j in range(7 - k):
                buf[far, :, lanes(j)] = jnp.zeros((LANE, LANE), F32)
            diagonal = dv_ref[BLOCKS.index((t, k))]
            block = jnp.where(cols > rows, pk_buf[n, :, lanes(k)].T, jnp.where(cols == rows, diagonal, 0.0))
            put(far, 7 - k, w_col, 7 - k, block)
            for j in range(k):
                put(far, 7 - k, w_col, 8 - k + j, pk_buf[n, :, lanes(j)])
            stores.append(send(far, 7 - k))
        for copy in stores:
            copy.wait()


def balance(name, t, ks, scalars, got, held, packed, dv, wr, wc, into=None, base=0):
    here, anywhere = pl.BlockSpec(memory_space=pltpu.VMEM), pl.BlockSpec(memory_space=pl.ANY)
    args = [scalars, got, held, packed, dv, wr, wc]
    in_specs = [pl.BlockSpec(memory_space=pltpu.SMEM), anywhere, anywhere, anywhere, here, here, here]
    aliases = {}
    if into is not None:
        aliases = {len(args): 0}
        in_specs.append(anywhere)
        args.append(into)
    count = 2 * len(ks)
    return pl.pallas_call(
        functools.partial(balance_kernel, t, ks, base),
        in_specs=in_specs,
        out_specs=anywhere,
        out_shape=jax.ShapeDtypeStruct(held.shape, F32),
        scratch_shapes=[
            pltpu.VMEM((count, LANE, 1024), F32),
            pltpu.VMEM((len(ks), LANE, 1024), F32),
            pltpu.SemaphoreType.DMA((count,)),
            pltpu.SemaphoreType.DMA((count,)),
        ],
        input_output_aliases=aliases,
        compiler_params=pltpu.CompilerParams(vmem_limit_bytes=VMEM_LIMIT),
        cost_estimate=pl.CostEstimate(flops=count << 18, bytes_accessed=count << 20, transcendentals=0),
        name=name,
    )(*args)


def local(held_tiles, placed, bin_mask, bias):
    move = moves(lax.axis_size("bins"))
    on_diagonal = lax.axis_index("diag") == 0
    live = bin_mask.astype(F32).reshape(2, 1024)
    scalars = jnp.concatenate([on_diagonal.astype(jnp.int32)[None], (placed == 1).astype(jnp.int32)])

    got = move["tiles"](held_tiles)
    ahead, most, last, dv = pack(held_tiles)

    here = lax.axis_index("bins")
    there = here ^ (lax.axis_size("bins") // 2)
    moved = placed[1] == 1

    def stored(lines):
        row_lines = [lines[3:4], jnp.where(moved, lines[4:5], lines[1:2])]
        next_lines = [lines[4:5], jnp.where(moved, lines[5:6], lines[2:3])]
        return jnp.concatenate(row_lines, axis=0), jnp.concatenate(next_lines, axis=0)

    def stored_parts(lines):
        rows, following = stored(lines)
        passed = move["core"](jnp.concatenate([rows, following], axis=0))
        row_w, col_w = jnp.where(on_diagonal, rows, passed[:2]), jnp.where(on_diagonal, rows, passed[2:])
        row_part, col_part = weighted_sums(scalars, held_tiles, row_w, col_w)
        off = move["core"](jnp.concatenate([row_part, col_part], axis=0))
        return row_part + col_part + off[:2], off[2:]

    def home_sums(mine, theirs):
        rows_d = [theirs[0:1], jnp.where(moved, theirs[1:2], mine[1:2])]
        rows_p = [mine[0:1], jnp.where(moved, mine[1:2], theirs[1:2])]
        cols_d = [theirs[2:3], jnp.where(moved, theirs[3:4], mine[3:4])]
        cols_p = [mine[2:3], jnp.where(moved, mine[3:4], theirs[3:4])]
        return rows_d, rows_p, cols_d, cols_p

    def sums_of(parts, which, cols_before, rows_after):
        rows, cols = parts[which], parts[2 + which]
        first = (there if which else here) == 0
        return jnp.concatenate(
            [rows[0] + jnp.where(first, 0.0, cols_before), rows[1] + cols[0], rows_after + cols[1]], axis=0
        )

    def neighbours(parts, count):
        rows_d, rows_p, cols_d, cols_p = parts
        cols_before = move["after"](jnp.concatenate([cols_d[1], cols_p[1]][:count], axis=0))
        rows_after = move["before"](jnp.concatenate([rows_d[0], rows_p[0]][:count], axis=0))
        return cols_before, rows_after

    after_live = move["before"](live[:1])
    live_lines = jnp.concatenate([live, after_live], axis=0)
    live_lines = jnp.concatenate([live_lines, move["across"](live_lines)], axis=0)
    live_lines, ahead = lax.optimization_barrier((live_lines, ahead))
    ahead = move["across"](ahead)

    rows, cols = stored_parts(live_lines)
    rows, cols, ahead = lax.optimization_barrier((rows, cols, ahead))
    line_1 = rows[:1] + rows[1:] + cols[:1] + cols[1:]
    mine = jnp.concatenate([rows, cols], axis=0)
    parts = home_sums(mine, move["across"](mine))
    ends = move["ends"](jnp.concatenate([parts[2][1], parts[0][0]], axis=0))
    ends, cols_before, rows_after = lax.optimization_barrier((ends, *neighbours(parts, 2)))
    cols_before = [cols_before[0:1], jnp.where(here == 0, ends[0:1], cols_before[1:2])]
    rows_after = [rows_after[0:1], jnp.where(there == lax.axis_size("bins") // 2 - 1, ends[1:2], rows_after[1:2])]
    sums_1 = jnp.concatenate([sums_of(parts, 0, cols_before[0], rows_after[0]), sums_of(parts, 1, cols_before[1], rows_after[1])], axis=0)

    rows, cols = stored_parts(jnp.where(live_lines > 0, 1.0 / sums_1, 0.0))
    totals = [line_1, rows[:1] + rows[1:] + cols[:1] + cols[1:], live[:1] + live[1:]]
    mine = jnp.concatenate([rows, cols, *totals, dv.reshape(1, 1024)], axis=0)
    theirs = move["across"](mine)
    parts = home_sums(mine, theirs)
    dv = theirs[7:8].reshape(8, 1, LANE)
    totals = jnp.sum((mine[4:7] + theirs[4:7]).reshape(3, 8, LANE), axis=1).reshape(1, 3 * LANE)
    beside, *around, most, last = lax.optimization_barrier(
        (move["beside"](totals), *neighbours(parts, 1), most, last)
    )
    most, last = move["across"](most), move["across"](last)
    totals = move["plane_sum"](totals + beside)
    sums_2 = sums_of(parts, 0, *around)
    totals = jnp.sum(totals.reshape(3, LANE), axis=1)
    scale = (totals[0] / totals[2]) * (totals[1] / totals[2])

    products = sums_1[:3] * sums_2
    weights = jnp.where(live_lines[:3] > 0, scale / products, 0.0)
    factor = jnp.where(live > 0, products[:2] / scale, 1.0)
    result = jnp.concatenate([weights, factor], axis=0)
    result = jnp.where(on_diagonal, result, move["core"](result))
    bias_out = bias.reshape(2, 1024) * result[3:]
    wr = result[:2].reshape(16, 1, LANE)
    wc = jnp.where(on_diagonal, result[:2], result[1:3]).reshape(2, 1, 1024)

    got, ahead, wr, wc, dv = lax.optimization_barrier((got, ahead, wr, wc, dv))
    out = balance("balance_ahead", 0, (0, 1), scalars, got, held_tiles, ahead, dv, wr, wc)
    out, most = lax.optimization_barrier((out, most))
    out = balance("balance_most", 0, (2, 3), scalars, got, held_tiles, most, dv, wr, wc, into=out)
    out = balance("balance_rest", 1, (1, 2, 3), scalars, got, held_tiles, most, dv, wr, wc, into=out, base=2)
    out, last = lax.optimization_barrier((out, last))
    out = balance("balance_last", 1, (0,), scalars, got, held_tiles, last, dv, wr, wc, into=out)
    return out, bias_out.reshape(2048)


def solution(mesh):
    placed = (P("bins", "diag", None, None), P("bins"), P("bins"), P("bins"))
    return jax.shard_map(
        local,
        mesh=mesh,
        in_specs=placed,
        out_specs=(P("bins", "diag", None, None), P("bins")),
        check_vma=False,
    )
```

```python
import functools

import jax
import jax.numpy as jnp
from jax import lax
from jax.experimental import pallas as pl
from jax.experimental.pallas import tpu as pltpu
from jax.sharding import PartitionSpec as P

AXES = ("bins", "diag")
F32 = jnp.float32
LANE = 128
VMEM_LIMIT = 48 * 1024 * 1024


def iotas():
    rows = lax.broadcasted_iota(jnp.int32, (LANE, LANE), 0)
    cols = lax.broadcasted_iota(jnp.int32, (LANE, LANE), 1)
    return rows, cols


def as_column(line):
    return jnp.broadcast_to(line, (LANE, LANE)).T


def lanes(k):
    return pl.ds(k * LANE, LANE)


def moves(n_bins):
    half = n_bins // 2
    chips = range(n_bins)

    def other(d):
        return (d + half) % n_bins

    def move(pairs, source_core, target_core):
        pairs = [(2 * s + source_core, 2 * t + target_core) for s, t in pairs]
        return lambda value: lax.ppermute(value, AXES, pairs)

    plane = max(n_bins // 4, 1)
    planes = [list(range(start, start + plane)) for start in range(0, n_bins, plane)]

    def plane_sum(value):
        spread = jnp.broadcast_to(value, (plane, value.shape[1]))
        seen = lax.all_to_all(spread, "bins", 0, 0, axis_index_groups=planes, tiled=True)
        return jnp.sum(seen, axis=0, keepdims=True)

    same = [(d, d) for d in chips]
    swap = [(d, other(d)) for d in chips]
    both_ways = [(2 * d, 2 * d + 1) for d in chips] + [(2 * d + 1, 2 * d) for d in chips]
    return dict(
        core=lambda value: lax.ppermute(value, AXES, both_ways),
        across=move(swap, 0, 0),
        tiles=move(swap, 1, 1),
        before=move([(d + 1, d) for d in chips[:-1]], 0, 0),
        after=move([(d, d + 1) for d in chips[:-1]], 0, 0),
        ends=move([(half - 1, 0), (half, n_bins - 1)], 0, 0),
        beside=move([(d, d ^ plane) for d in chips], 0, 0),
        plane_sum=plane_sum,
    )


BLOCKS = [(0, 0), (0, 1), (0, 2), (0, 3), (1, 1), (1, 2), (1, 3), (1, 0)]
SENT = (1, 6, 1)


def pack_kernel(held_ref, *refs):
    out_refs, (dv_ref, near_buf, far_buf, in_sem, out_sem) = refs[: len(SENT)], refs[len(SENT) :]
    rows, cols = iotas()
    count = len(BLOCKS)
    targets = [ref.at[pl.ds(j * LANE, LANE), :] for ref, blocks in zip(out_refs, SENT) for j in range(blocks)]

    def source(t, b, start, width):
        return held_ref.at[t, 0, pl.ds(b * LANE, LANE), pl.ds(start * LANE, width * LANE)]

    def near(n, start, width):
        return near_buf.at[n, :, pl.ds(start * LANE, width * LANE)]

    loads = [[] for _ in BLOCKS]
    for n, (t, k) in enumerate(BLOCKS):
        loads[n].append(pltpu.make_async_copy(source(t, 7 - k, 7 - k, 1), far_buf.at[n], in_sem.at[n]))
        loads[n].append(pltpu.make_async_copy(source(t, k, k, 8 - k), near(n, k, 8 - k), in_sem.at[count + n]))
        if k:
            loads[n].append(pltpu.make_async_copy(source(t, 7 - k, 8 - k, k), near(n, 0, k), in_sem.at[2 * count + n]))
        for copy in loads[n]:
            copy.start()
    stores = []
    for n, (t, k) in enumerate(BLOCKS):
        for copy in loads[n]:
            copy.wait()
        far = far_buf[n]
        block = near(n, k, 1)
        block[...] = jnp.where(cols >= rows, block[...], far.T)
        dv_ref[n] = jnp.sum(jnp.where(cols == rows, far, 0.0), axis=0, keepdims=True)
        stores.append(pltpu.make_async_copy(near_buf.at[n], targets[n], out_sem.at[n]))
        stores[-1].start()
    for copy in stores:
        copy.wait()


def pack(held):
    return pl.pallas_call(
        pack_kernel,
        in_specs=[pl.BlockSpec(memory_space=pl.ANY)],
        out_specs=[pl.BlockSpec(memory_space=pltpu.HBM)] * len(SENT) + [pl.BlockSpec(memory_space=pltpu.VMEM)],
        out_shape=[jax.ShapeDtypeStruct((blocks * LANE, 1024), F32) for blocks in SENT]
        + [jax.ShapeDtypeStruct((8, 1, LANE), F32)],
        scratch_shapes=[
            pltpu.VMEM((8, LANE, 1024), F32),
            pltpu.VMEM((8, LANE, LANE), F32),
            pltpu.SemaphoreType.DMA((24,)),
            pltpu.SemaphoreType.DMA((8,)),
        ],
        compiler_params=pltpu.CompilerParams(vmem_limit_bytes=VMEM_LIMIT),
        cost_estimate=pl.CostEstimate(flops=1 << 20, bytes_accessed=8 << 20, transcendentals=0),
        name="pack_triangles",
    )(held)


def sums_kernel(sc_ref, held_ref, a_ref, b_ref, row_ref, col_ref, buf, sem):
    rows, cols = iotas()

    def add_up(triangle):
        copies = []
        for n in range(16):
            t, b = n // 8, n % 8
            near = pl.ds(b * LANE, LANE)
            kept = pl.ds(b * LANE, (8 - b) * LANE) if triangle else pl.ds(0, 1024)
            copies.append(pltpu.make_async_copy(held_ref.at[t, 0, near, kept], buf.at[t, near, kept], sem.at[n]))
            copies[-1].start()
        for t in range(2):
            below = [jnp.zeros((8, LANE), F32) for _ in range(8)]
            for b in range(8):
                copies[8 * t + b].wait()
                a_line = a_ref[t, :, lanes(b)]
                a_col = as_column(a_line)
                across = jnp.zeros((LANE, LANE), F32)
                for k in range(b if triangle else 0, 8):
                    right = down = buf[t, pl.ds(b * LANE, LANE), lanes(k)]
                    if triangle and k == b:
                        right, down = jnp.where(cols >= rows, right, 0.0), jnp.where(cols > rows, down, 0.0)
                    across += right * b_ref[t, :, lanes(k)]
                    below[k] += jnp.sum((down * a_col).reshape(LANE // 8, 8, LANE), axis=0)
                row_ref[t, :, lanes(b)] = jnp.sum(across.T, axis=0, keepdims=True) * a_line
            for k in range(8):
                col_ref[t, :, lanes(k)] = jnp.sum(below[k], axis=0, keepdims=True) * b_ref[t, :, lanes(k)]

    @pl.when(sc_ref[0] == 1)
    def _():
        add_up(True)

    @pl.when(sc_ref[0] == 0)
    def _():
        add_up(False)


def weighted_sums(scalars, held, row_w, col_w):
    shape = jax.ShapeDtypeStruct((2, 1, 1024), F32)
    here = pl.BlockSpec(memory_space=pltpu.VMEM)
    row_part, col_part = pl.pallas_call(
        sums_kernel,
        in_specs=[pl.BlockSpec(memory_space=pltpu.SMEM), pl.BlockSpec(memory_space=pl.ANY), here, here],
        out_specs=[here, here],
        out_shape=[shape, shape],
        scratch_shapes=[pltpu.VMEM((2, 1024, 1024), F32), pltpu.SemaphoreType.DMA((16,))],
        compiler_params=pltpu.CompilerParams(vmem_limit_bytes=VMEM_LIMIT),
        cost_estimate=pl.CostEstimate(flops=8 << 20, bytes_accessed=8 << 20, transcendentals=0),
        name="weighted_sums",
    )(scalars, held, row_w.reshape(2, 1, 1024), col_w.reshape(2, 1, 1024))
    return row_part.reshape(2, 1024), col_part.reshape(2, 1024)


def balance_kernel(t, ks, base, sc_ref, got_ref, held_ref, pk_ref, dv_ref, wr_ref, wc_ref, *rest):
    out_ref, buf, pk_buf, in_sem, out_sem = rest[-5:]
    rows, cols = iotas()
    on_diagonal = sc_ref[0] == 1
    moved = sc_ref[1 + t] == 1
    blocks = [b for k in ks for b in (k, 7 - k)]

    def place(ref, b):
        return ref.at[t, 0, pl.ds(b * LANE, LANE), :]

    def put(i, b, w_col, j, x):
        buf[i, :, lanes(j)] = x * w_col * wc_ref[t, :, lanes(j)]

    def send(i, b):
        copy = pltpu.make_async_copy(buf.at[i], place(out_ref, b), out_sem.at[i])
        copy.start()
        return copy

    def from_rows(ref, masked):
        loads = [pltpu.make_async_copy(place(ref, b), buf.at[i], in_sem.at[i]) for i, b in enumerate(blocks)]
        for copy in loads:
            copy.start()
        stores = []
        for i, b in enumerate(blocks):
            loads[i].wait()
            w_col = as_column(wr_ref[t * 8 + b])
            for j in range(8):
                x = buf[i, :, lanes(j)]
                put(i, b, w_col, j, jnp.where(cols - rows >= (b - j) * LANE, x, 0.0) if masked else x)
            stores.append(send(i, b))
        for copy in stores:
            copy.wait()

    @pl.when(moved & jnp.logical_not(on_diagonal))
    def _():
        from_rows(got_ref, False)

    @pl.when(jnp.logical_not(moved) & jnp.logical_not(on_diagonal))
    def _():
        from_rows(held_ref, False)

    @pl.when(jnp.logical_not(moved) & on_diagonal)
    def _():
        from_rows(held_ref, True)

    @pl.when(moved & on_diagonal)
    def _():
        loads = [
            pltpu.make_async_copy(pk_ref.at[pl.ds((base + n) * LANE, LANE), :], pk_buf.at[n], in_sem.at[n])
            for n in range(len(ks))
        ]
        for copy in loads:
            copy.start()
        stores = []
        for n, k in enumerate(ks):
            loads[n].wait()
            near, far = 2 * n, 2 * n + 1
            w_col = as_column(wr_ref[t * 8 + k])
            for j in range(k):
                buf[near, :, lanes(j)] = jnp.zeros((LANE, LANE), F32)
            put(near, k, w_col, k, jnp.where(cols >= rows, pk_buf[n, :, lanes(k)], 0.0))
            for j in range(k + 1, 8):
                put(near, k, w_col, j, pk_buf[n, :, lanes(j)])
            stores.append(send(near, k))
            w_col = as_column(wr_ref[t * 8 + 7 - k])
            for j in range(7 - k):
                buf[far, :, lanes(j)] = jnp.zeros((LANE, LANE), F32)
            diagonal = dv_ref[BLOCKS.index((t, k))]
            block = jnp.where(cols > rows, pk_buf[n, :, lanes(k)].T, jnp.where(cols == rows, diagonal, 0.0))
            put(far, 7 - k, w_col, 7 - k, block)
            for j in range(k):
                put(far, 7 - k, w_col, 8 - k + j, pk_buf[n, :, lanes(j)])
            stores.append(send(far, 7 - k))
        for copy in stores:
            copy.wait()


def balance(name, t, ks, scalars, got, held, packed, dv, wr, wc, into=None, base=0):
    here, anywhere = pl.BlockSpec(memory_space=pltpu.VMEM), pl.BlockSpec(memory_space=pl.ANY)
    args = [scalars, got, held, packed, dv, wr, wc]
    in_specs = [pl.BlockSpec(memory_space=pltpu.SMEM), anywhere, anywhere, anywhere, here, here, here]
    aliases = {}
    if into is not None:
        aliases = {len(args): 0}
        in_specs.append(anywhere)
        args.append(into)
    count = 2 * len(ks)
    return pl.pallas_call(
        functools.partial(balance_kernel, t, ks, base),
        in_specs=in_specs,
        out_specs=anywhere,
        out_shape=jax.ShapeDtypeStruct(held.shape, F32),
        scratch_shapes=[
            pltpu.VMEM((count, LANE, 1024), F32),
            pltpu.VMEM((len(ks), LANE, 1024), F32),
            pltpu.SemaphoreType.DMA((count,)),
            pltpu.SemaphoreType.DMA((count,)),
        ],
        input_output_aliases=aliases,
        compiler_params=pltpu.CompilerParams(vmem_limit_bytes=VMEM_LIMIT),
        cost_estimate=pl.CostEstimate(flops=count << 18, bytes_accessed=count << 20, transcendentals=0),
        name=name,
    )(*args)


def local(held_tiles, placed, bin_mask, bias):
    move = moves(lax.axis_size("bins"))
    on_diagonal = lax.axis_index("diag") == 0
    live = bin_mask.astype(F32).reshape(2, 1024)
    scalars = jnp.concatenate([on_diagonal.astype(jnp.int32)[None], (placed == 1).astype(jnp.int32)])

    got = move["tiles"](held_tiles)
    ahead, most, last, dv = pack(held_tiles)

    here = lax.axis_index("bins")
    there = here ^ (lax.axis_size("bins") // 2)
    moved = placed[1] == 1

    def stored(lines):
        row_lines = [lines[3:4], jnp.where(moved, lines[4:5], lines[1:2])]
        next_lines = [lines[4:5], jnp.where(moved, lines[5:6], lines[2:3])]
        return jnp.concatenate(row_lines, axis=0), jnp.concatenate(next_lines, axis=0)

    def stored_parts(lines):
        rows, following = stored(lines)
        passed = move["core"](jnp.concatenate([rows, following], axis=0))
        row_w, col_w = jnp.where(on_diagonal, rows, passed[:2]), jnp.where(on_diagonal, rows, passed[2:])
        row_part, col_part = weighted_sums(scalars, held_tiles, row_w, col_w)
        off = move["core"](jnp.concatenate([row_part, col_part], axis=0))
        return row_part + col_part + off[:2], off[2:]

    def home_sums(mine, theirs):
        rows_d = [theirs[0:1], jnp.where(moved, theirs[1:2], mine[1:2])]
        rows_p = [mine[0:1], jnp.where(moved, mine[1:2], theirs[1:2])]
        cols_d = [theirs[2:3], jnp.where(moved, theirs[3:4], mine[3:4])]
        cols_p = [mine[2:3], jnp.where(moved, mine[3:4], theirs[3:4])]
        return rows_d, rows_p, cols_d, cols_p

    def sums_of(parts, which, cols_before, rows_after):
        rows, cols = parts[which], parts[2 + which]
        first = (there if which else here) == 0
        return jnp.concatenate(
            [rows[0] + jnp.where(first, 0.0, cols_before), rows[1] + cols[0], rows_after + cols[1]], axis=0
        )

    def neighbours(parts, count):
        rows_d, rows_p, cols_d, cols_p = parts
        cols_before = move["after"](jnp.concatenate([cols_d[1], cols_p[1]][:count], axis=0))
        rows_after = move["before"](jnp.concatenate([rows_d[0], rows_p[0]][:count], axis=0))
        return cols_before, rows_after

    after_live = move["before"](live[:1])
    live_lines = jnp.concatenate([live, after_live], axis=0)
    live_lines = jnp.concatenate([live_lines, move["across"](live_lines)], axis=0)
    live_lines, ahead = lax.optimization_barrier((live_lines, ahead))
    ahead = move["across"](ahead)

    rows, cols = stored_parts(live_lines)
    rows, cols, ahead = lax.optimization_barrier((rows, cols, ahead))
    line_1 = rows[:1] + rows[1:] + cols[:1] + cols[1:]
    mine = jnp.concatenate([rows, cols], axis=0)
    parts = home_sums(mine, move["across"](mine))
    ends = move["ends"](jnp.concatenate([parts[2][1], parts[0][0]], axis=0))
    ends, cols_before, rows_after = lax.optimization_barrier((ends, *neighbours(parts, 2)))
    cols_before = [cols_before[0:1], jnp.where(here == 0, ends[0:1], cols_before[1:2])]
    rows_after = [rows_after[0:1], jnp.where(there == lax.axis_size("bins") // 2 - 1, ends[1:2], rows_after[1:2])]
    sums_1 = jnp.concatenate([sums_of(parts, 0, cols_before[0], rows_after[0]), sums_of(parts, 1, cols_before[1], rows_after[1])], axis=0)

    rows, cols = stored_parts(jnp.where(live_lines > 0, 1.0 / sums_1, 0.0))
    totals = [line_1, rows[:1] + rows[1:] + cols[:1] + cols[1:], live[:1] + live[1:]]
    mine = jnp.concatenate([rows, cols, *totals, dv.reshape(1, 1024)], axis=0)
    theirs = move["across"](mine)
    parts = home_sums(mine, theirs)
    dv = theirs[7:8].reshape(8, 1, LANE)
    totals = jnp.sum((mine[4:7] + theirs[4:7]).reshape(3, 8, LANE), axis=1).reshape(1, 3 * LANE)
    beside, *around, most, last = lax.optimization_barrier(
        (move["beside"](totals), *neighbours(parts, 1), most, last)
    )
    most, last = move["across"](most), move["across"](last)
    totals = move["plane_sum"](totals + beside)
    sums_2 = sums_of(parts, 0, *around)
    totals = jnp.sum(totals.reshape(3, LANE), axis=1)
    scale = (totals[0] / totals[2]) * (totals[1] / totals[2])

    products = sums_1[:3] * sums_2
    weights = jnp.where(live_lines[:3] > 0, scale / products, 0.0)
    factor = jnp.where(live > 0, products[:2] / scale, 1.0)
    result = jnp.concatenate([weights, factor], axis=0)
    result = jnp.where(on_diagonal, result, move["core"](result))
    bias_out = bias.reshape(2, 1024) * result[3:]
    wr = result[:2].reshape(16, 1, LANE)
    wc = jnp.where(on_diagonal, result[:2], result[1:3]).reshape(2, 1, 1024)

    got, ahead, wr, wc, dv = lax.optimization_barrier((got, ahead, wr, wc, dv))
    out = balance("balance_ahead", 0, (0,), scalars, got, held_tiles, ahead, dv, wr, wc)
    out, most = lax.optimization_barrier((out, most))
    out = balance("balance_most", 0, (1, 2, 3), scalars, got, held_tiles, most, dv, wr, wc, into=out)
    out = balance("balance_rest", 1, (1, 2, 3), scalars, got, held_tiles, most, dv, wr, wc, into=out, base=3)
    out, last = lax.optimization_barrier((out, last))
    out = balance("balance_last", 1, (0,), scalars, got, held_tiles, last, dv, wr, wc, into=out)
    return out, bias_out.reshape(2048)


def solution(mesh):
    placed = (P("bins", "diag", None, None), P("bins"), P("bins"), P("bins"))
    return jax.shard_map(
        local,
        mesh=mesh,
        in_specs=placed,
        out_specs=(P("bins", "diag", None, None), P("bins")),
        check_vma=False,
    )
```
